32 devices in a mesh: grp: 4 (over z), ctx: 8 (over y, x, core).
Axes of the slice: x: 2, y: 2, z: 4, core: 2. Of those that a mesh axis runs over, the one named last changes fastest.
Arguments:
- queries: bfloat16 [12288, 1024], P(('grp', 'ctx')), may hold values from -10 to 10
- keys_cache: bfloat16 [4096, 128, 128], P(('grp', 'ctx')), may hold values from -8 to 8
- values_cache: bfloat16 [4096, 128, 128], P(('grp', 'ctx')), may hold values from -6 to 6
- block_list: int32 [96, 36], P(('grp', 'ctx')), may hold values from 0 to 4095, as said below
- page_table: int32 [4096], replicated, may hold values from 0 to 4095, as said below
Outputs:
- attended: bfloat16 [12288, 1024], P(('grp', 'ctx'))
The draws below stay inside these ranges and needn't reach their ends.
Inputs may be any that keep to these rules, and one draw needn't show every extreme that they name: `block_list`: each tile's 36 listed blocks are distinct. Page p is row p of keys_cache and values_cache. Through page_table, each tile lists exactly 9 blocks stored on the devices of each index of grp. Over the 3 tiles of one device and one index of grp, at most 7 listed blocks are stored on any one device, and in every draw, for every device and every group, some device of that group stores exactly 7 of them. `page_table`: each page once.
All inputs are finite; a program needn't handle non-finite values.
Results may differ from the reference program's by a relative error of at most 0.0045.
Values may be sent and summed in bfloat16 or wider, within the bound.
No kernel may reach another device: no remote copies, remote signals or barrier semaphores. Data moves between devices by JAX's collectives and lax.ppermute only.
A program may use at most 192 MiB of HBM per device.

```python
import jax
import jax.numpy as jnp
from jax import lax

HD = 128
HEADS = 8
BLOCK = 128
NB = 36
TILE_DEV = 3
BLK_DEV = 128
PER_GRP = 9
CAP = 7
TILES = 96
TOKENS = 12288
PAGES = 4096


def draw_queries(key, part):
    sub_key = jax.random.fold_in(key, 11)
    filled = jnp.clip(2.5 * jax.random.normal(sub_key, (TOKENS, HEADS * HD), jnp.float32), -10.0, 10.0)
    return filled.astype(jnp.bfloat16)


def draw_keys_cache(key, part):
    sub_key = jax.random.fold_in(key, 23)
    filled = jnp.clip(jax.random.normal(sub_key, (PAGES, BLOCK, HD), jnp.float32), -6.0, 6.0)
    return filled.astype(jnp.bfloat16)


def listing(key):
    groups = NB // PER_GRP
    devices = PAGES // BLK_DEV
    owners_count = devices // groups
    requests = TILE_DEV * PER_GRP
    slot_count = owners_count * CAP
    base_key = jax.random.fold_in(key, 505)
    page_table = jax.random.permutation(jax.random.fold_in(base_key, 1), PAGES).astype(jnp.int32)
    busiest = jax.random.randint(jax.random.fold_in(base_key, 2), (groups,), 0, owners_count)
    jitter = jax.random.randint(jax.random.fold_in(base_key, 3), (devices, groups, slot_count), 0, 1 << 20)
    slot_ids = jnp.arange(slot_count, dtype=jnp.int32)
    owner_of = slot_ids // CAP
    is_hot = (owner_of[None, None, :] == busiest[None, :, None]).astype(jnp.int32)
    ranked = (jitter + is_hot * (1 << 20)) * slot_count + slot_ids[None, None, :]
    ranking = jnp.argsort(ranked, axis=-1)
    chosen_owner = owner_of[ranking[:, :, :requests - CAP]]
    hot_owner = jnp.broadcast_to(busiest[None, :, None], (devices, groups, CAP))
    owners = jnp.concatenate([hot_owner, chosen_owner], axis=-1)
    jitter_two = jax.random.randint(jax.random.fold_in(base_key, 4), (devices, groups, requests), 0, 1 << 20)
    shuffle = jnp.argsort(jitter_two * requests + jnp.arange(requests, dtype=jnp.int32)[None, None, :], axis=-1)
    owners = jnp.take_along_axis(owners, shuffle, axis=-1).reshape(devices, groups, TILE_DEV, PER_GRP)
    offset = jax.random.randint(jax.random.fold_in(base_key, 5), (devices, groups, TILE_DEV, 1), 0, BLK_DEV)
    in_device = (offset + 7 * jnp.arange(PER_GRP, dtype=jnp.int32)[None, None, None, :]) % BLK_DEV
    group_index = jnp.arange(groups, dtype=jnp.int32)[None, :, None, None]
    page_ids = (group_index * owners_count + owners) * BLK_DEV + in_device
    page_ids = page_ids.transpose(0, 2, 1, 3).reshape(TILES, NB)
    jitter_three = jax.random.randint(jax.random.fold_in(base_key, 6), (TILES, NB), 0, 1 << 20)
    spread = jnp.argsort(jitter_three * NB + jnp.arange(NB, dtype=jnp.int32)[None, :], axis=-1)
    page_ids = jnp.take_along_axis(page_ids, spread, axis=-1)
    inverse = jnp.zeros((PAGES,), jnp.int32).at[page_table].set(jnp.arange(PAGES, dtype=jnp.int32))
    block_list = inverse[page_ids].astype(jnp.int32)
    return (block_list, page_table)


def draw_block_list(key, part):
    return listing(key)[0]


def draw_page_table(key, part):
    return listing(key)[1]


def block_levels(key, dims, pieces, least, high):
    def one(dim, blocks):
        steps = jax.random.uniform(jax.random.fold_in(jax.random.fold_in(key, 6), dim), (blocks,), jnp.float32, least / len(pieces), high / len(pieces))
        return jnp.repeat(jnp.exp(steps), dims[dim] // blocks).reshape((-1,) + (1,) * (len(dims) - dim - 1))

    loudness = one(*pieces[0])
    for cut in pieces[1:]:
        loudness = loudness * one(*cut)
    return loudness


def scatter_about(rng, extent, scale, limit, pieces=(), held_as=jnp.bfloat16):
    values = scale * jax.random.normal(rng, extent, jnp.float32)
    if pieces:
        values = values * block_levels(rng, extent, pieces, -0.22, 0.18)
    return jnp.clip(values, -limit, limit).astype(held_as)


def setup_inputs(seed: int = 0) -> dict:
    streams_of = jax.random.split(jax.random.key(seed), 6)
    queries = draw_queries(jax.random.fold_in(streams_of[5], 71), 0)
    keys_cache = draw_keys_cache(jax.random.fold_in(streams_of[5], 71), 0)
    values_cache = scatter_about(streams_of[2], (PAGES, BLOCK, HD), 1.0, 6.0, ((0, 32),))
    block_list = draw_block_list(jax.random.fold_in(streams_of[5], 71), 0)
    page_table = draw_page_table(jax.random.fold_in(streams_of[5], 71), 0)
    return {"queries": queries, "keys_cache": keys_cache, "values_cache": values_cache, "block_list": block_list, "page_table": page_table}


def reference(queries, keys_cache, values_cache, block_list, page_table):
    scaling = HD ** -0.5
    query_tiles = queries.reshape(TILES, BLOCK, HEADS, HD)

    def attend_tile(operands):
        tile_rows, listed = operands
        page_ids = page_table[listed].astype(jnp.int32)
        tile_keys = keys_cache[page_ids].reshape(NB * BLOCK, HD)
        tile_values = values_cache[page_ids].reshape(NB * BLOCK, HD)
        stacked = tile_rows.transpose(1, 0, 2).reshape(HEADS * BLOCK, HD)
        scores = jnp.dot(stacked, tile_keys.T, preferred_element_type=jnp.float32) * scaling
        largest = jnp.max(scores, axis=1, keepdims=True)
        weights = jnp.exp(scores - largest)
        denominator = jnp.sum(weights, axis=1)
        summed = jnp.dot(weights.astype(jnp.bfloat16), tile_values, preferred_element_type=jnp.float32)
        result = summed / denominator[:, None]
        result = result.reshape(HEADS, BLOCK, HD).transpose(1, 0, 2).reshape(BLOCK, HEADS * HD)
        return result.astype(jnp.bfloat16)

    attended = lax.map(attend_tile, (query_tiles, block_list))
    return attended.reshape(TOKENS, HEADS * HD)
```

```python
import functools
import math

import jax
import jax.numpy as jnp
from jax import lax
from jax.experimental import pallas as pl
from jax.experimental.pallas import tpu as pltpu
from jax.sharding import PartitionSpec as P

LANES = 128
LOG2E = math.log2(math.e)


def shifted(block, axis, distance):
    devices = range(lax.axis_size(axis))
    route = [((i - distance) % len(devices), i) for i in devices]
    return lax.ppermute(block, axis, route)


def before(first, second):
    return lax.optimization_barrier((first, second))


def plan_body(groups, ctx_count, cap, shift, place, lists, sends, picks):
    group, here = place[0], place[1]
    rows = groups * ctx_count
    lane = lax.broadcasted_iota(jnp.int32, (rows, LANES), 1)
    earlier = (
        lax.broadcasted_iota(jnp.int32, (LANES, LANES), 0)
        < lax.broadcasted_iota(jnp.int32, (LANES, LANES), 1)
    ).astype(jnp.float32).astype(jnp.bfloat16)

    def rank_of(mask):
        ones = jnp.where(mask, 1.0, 0.0).astype(jnp.bfloat16)
        return jnp.dot(ones, earlier, preferred_element_type=jnp.float32).astype(jnp.int32)

    pages = lists[...]
    mine = (pages >> shift) == group * ctx_count + here
    rank = rank_of(mine)
    within = pages & ((1 << shift) - 1)
    found = jnp.full((rows, LANES), -1, jnp.int32)
    for k in range(cap):
        chosen = jnp.max(jnp.where(mine & (rank == k), within, -1), axis=1, keepdims=True)
        found = jnp.where(lane == k, chosen, found)
    sends[...] = found

    owner = lax.broadcasted_iota(jnp.int32, (ctx_count, LANES), 0)
    order = lax.broadcasted_iota(jnp.int32, (LANES, LANES), 0)
    for home in range(groups):
        listed = lists[pl.ds(home * ctx_count + here, 1), :]
        member = (jnp.broadcast_to(listed, (ctx_count, LANES)) >> shift) == group * ctx_count + owner
        slot = jnp.where(member, owner * cap + rank_of(member), 0)
        slot = jnp.sum(slot, axis=0, keepdims=True)
        inside = jnp.broadcast_to((listed >> shift) // ctx_count == group, (8, LANES))
        ordinal = rank_of(inside)[0:1]
        here_row = jnp.broadcast_to(ordinal, (LANES, LANES)) == order
        here_row = here_row & (jnp.broadcast_to(inside[0:1].astype(jnp.int32), (LANES, LANES)) > 0)
        onehot = jnp.where(here_row, 1.0, 0.0).astype(jnp.bfloat16)
        picked = lax.dot_general(
            jnp.broadcast_to(slot, (8, LANES)).astype(jnp.float32).astype(jnp.bfloat16),
            onehot,
            (((1,), (1,)), ((), ())),
            preferred_element_type=jnp.float32,
        )
        picks[home : home + 1, :] = picked[0:1].astype(jnp.int32)


def make_plan(place, lists, groups, ctx_count, cap, pages_here):
    rows = groups * ctx_count
    shift = pages_here.bit_length() - 1
    return pl.pallas_call(
        functools.partial(plan_body, groups, ctx_count, cap, shift),
        out_shape=(
            jax.ShapeDtypeStruct((rows, LANES), jnp.int32),
            jax.ShapeDtypeStruct((groups, LANES), jnp.int32),
        ),
        in_specs=[
            pl.BlockSpec(memory_space=pltpu.SMEM),
            pl.BlockSpec(memory_space=pltpu.VMEM),
        ],
        name="plan",
    )(place, lists)


def collect_body(ctx_count, cap, home, sends, keys, values, out, sem):
    first = home[0] * ctx_count

    def copies(i):
        page = sends[first + i // cap, i % cap]
        return page, (
            pltpu.make_async_copy(keys.at[page], out.at[i, 0], sem),
            pltpu.make_async_copy(values.at[page], out.at[i, 1], sem),
        )

    def begin(i, carry):
        page, pair = copies(i)

        @pl.when(page >= 0)
        def _():
            pair[0].start()
            pair[1].start()

        return carry

    def finish(i, carry):
        page = sends[first + i // cap, i % cap]

        @pl.when(page >= 0)
        def _():
            pltpu.make_async_copy(keys.at[0], out.at[0, 0], sem).wait()
            pltpu.make_async_copy(values.at[0], out.at[0, 1], sem).wait()

        return carry

    lax.fori_loop(0, ctx_count * cap, begin, 0)
    lax.fori_loop(0, ctx_count * cap, finish, 0)


def collect(home, sends, keys, values, ctx_count, cap):
    _, block, hd = keys.shape
    slots = ctx_count * cap
    return pl.pallas_call(
        functools.partial(collect_body, ctx_count, cap),
        out_shape=jax.ShapeDtypeStruct((slots, 2, block, hd), keys.dtype),
        grid_spec=pltpu.PrefetchScalarGridSpec(
            num_scalar_prefetch=2,
            grid=(),
            in_specs=[pl.BlockSpec(memory_space=pl.ANY)] * 2,
            out_specs=pl.BlockSpec(memory_space=pl.ANY),
            scratch_shapes=[pltpu.SemaphoreType.DMA(())],
        ),
        name="collect",
    )(home, sends, keys, values)


def attend_body(per_grp, heads, others, home, picks, q, fetched, *rest):
    if others:
        parts, sizes, out, kbuf, vbuf, sem = rest
    else:
        out, size_out, kbuf, vbuf, sem = rest
    tile = pl.program_id(0)
    tiles = pl.num_programs(0)
    block = q.shape[0]
    hd = q.shape[1] // heads

    def copies(which, slot):
        pairs = []
        for j in range(per_grp):
            page = picks[home[0], which * per_grp + j]
            span = pl.ds(j * block, block)
            pairs.append(pltpu.make_async_copy(fetched.at[page, 0], kbuf.at[slot, span], sem.at[slot]))
            pairs.append(
                pltpu.make_async_copy(fetched.at[page, 1], vbuf.at[slot, span, pl.ds(0, hd)], sem.at[slot])
            )
        return pairs

    slot = lax.rem(tile, 2)

    @pl.when(tile == 0)
    def _():
        vbuf[:, :, hd:] = jnp.ones((2, per_grp * block, hd), vbuf.dtype)
        for copy in copies(0, 0):
            copy.start()

    @pl.when(tile + 1 < tiles)
    def _():
        for copy in copies(tile + 1, 1 - slot):
            copy.start()

    for copy in copies(tile, slot):
        copy.wait()

    factor = hd ** (-0.5) * LOG2E
    diagonal = lax.broadcasted_iota(jnp.int32, (block, block), 0) == lax.broadcasted_iota(
        jnp.int32, (block, block), 1
    )
    pair = 2
    if others:
        size_rows = [sizes[g] for g in range(others)]
        size_cols = [jnp.transpose(rows) for rows in size_rows]
    for first in range(0, heads, pair):
        rows = jnp.concatenate([q[:, (first + i) * hd : (first + i + 1) * hd] for i in range(pair)], axis=0)
        scores = lax.dot_general(
            rows, kbuf[slot], (((1,), (1,)), ((), ())), preferred_element_type=jnp.float32
        )
        top = jnp.max(scores, axis=1, keepdims=True)
        weights = jnp.exp2((scores - top) * factor).astype(jnp.bfloat16)
        summed = jnp.dot(weights, vbuf[slot], preferred_element_type=jnp.float32)
        for i in range(pair):
            span = slice(i * block, (i + 1) * block)
            col = slice((first + i) * hd, (first + i + 1) * hd)
            total = summed[span, hd:]
            mine = summed[span, :hd] / total
            size = top[span] * factor + jnp.log2(total)
            if others:
                theirs = [
                    jnp.broadcast_to(size_cols[g][:, first + i : first + i + 1], (block, hd))
                    for g in range(others)
                ]
                peak = size
                for one in theirs:
                    peak = jnp.maximum(peak, one)
                share = jnp.exp2(size - peak)
                whole = share
                merged = mine * share
                for g in range(others):
                    share = jnp.exp2(theirs[g] - peak)
                    whole = whole + share
                    merged = merged + parts[g, :, col].astype(jnp.float32) * share
                out[:, col] = (merged / whole).astype(out.dtype)
            else:
                out[:, col] = mine.astype(out.dtype)
                size_out[0, first + i : first + i + 1, :] = jnp.sum(
                    jnp.where(diagonal, size, 0.0), axis=0, keepdims=True
                )


def attend(home, picks, q, fetched, per_grp, heads, parts=None, sizes=None):
    tokens, width = q.shape
    block, hd = fetched.shape[2:]
    tiles = tokens // block
    others = 0 if parts is None else parts.shape[0]
    q_spec = pl.BlockSpec((block, width), lambda t, *_: (t, 0))
    size_shape = (heads, block)
    in_specs = [q_spec, pl.BlockSpec(memory_space=pl.ANY)]
    operands = [q, fetched]
    out_shape = [jax.ShapeDtypeStruct((tokens, width), q.dtype)]
    out_specs = [q_spec]
    if others:
        in_specs += [
            pl.BlockSpec((others, block, width), lambda t, *_: (0, t, 0)),
            pl.BlockSpec((others, None) + size_shape, lambda t, *_: (0, t, 0, 0)),
        ]
        operands += [parts, sizes]
    else:
        out_shape.append(jax.ShapeDtypeStruct((tiles,) + size_shape, jnp.float32))
        out_specs.append(pl.BlockSpec((1,) + size_shape, lambda t, *_: (t, 0, 0)))
    return pl.pallas_call(
        functools.partial(attend_body, per_grp, heads, others),
        out_shape=tuple(out_shape),
        grid_spec=pltpu.PrefetchScalarGridSpec(
            num_scalar_prefetch=2,
            grid=(tiles,),
            in_specs=in_specs,
            out_specs=tuple(out_specs),
            scratch_shapes=[
                pltpu.VMEM((2, per_grp * block, hd), q.dtype),
                pltpu.VMEM((2, per_grp * block, 2 * hd), q.dtype),
                pltpu.SemaphoreType.DMA((2,)),
            ],
        ),
        compiler_params=pltpu.CompilerParams(vmem_limit_bytes=48 * 1024 * 1024),
        name="attend_last" if others else "attend",
    )(home, picks, *operands)


def on_device(queries, keys_cache, values_cache, block_list, page_table):
    groups = lax.axis_size("grp")
    ctx_count = lax.axis_size("ctx")
    tile_count, listed = block_list.shape
    pages_here, block, hd = keys_cache.shape
    heads = queries.shape[1] // hd
    per_grp = listed // groups
    cap = max(3, (2 * tile_count * per_grp + ctx_count - 1) // ctx_count)
    group_here = lax.axis_index("grp")
    ctx_here = lax.axis_index("ctx")
    place = jnp.stack([group_here, ctx_here]).astype(jnp.int32)

    page_ids = page_table[block_list].reshape(1, tile_count * listed)
    page_ids = jnp.pad(page_ids, ((0, 0), (0, LANES - tile_count * listed)), constant_values=-1)
    everywhere = jnp.broadcast_to(page_ids, (groups * ctx_count, LANES))
    lists = lax.all_to_all(everywhere, ("grp", "ctx"), split_axis=0, concat_axis=0, tiled=True)
    sends, picks = make_plan(place, lists, groups, ctx_count, cap, pages_here)

    shifts = [s for s in (2, 1, 3) if s < groups] + [s for s in range(4, groups)]
    sends, queries_out = before(sends, queries)
    homes = {s: ((group_here - s) % groups).astype(jnp.int32).reshape(1) for s in shifts + [0]}
    visiting = {s: shifted(queries_out, "grp", s) for s in shifts}
    visiting[0] = queries

    def fetch(s):
        gathered = collect(homes[s], sends, keys_cache, values_cache, ctx_count, cap)
        return lax.all_to_all(gathered, "ctx", split_axis=0, concat_axis=0, tiled=True)

    parts, sizes = [], []
    for s in shifts:
        part, size = attend(homes[s], picks, visiting[s], fetch(s), per_grp, heads)
        parts.append(shifted(part, "grp", -s))
        sizes.append(shifted(size, "grp", -s))
    return attend(
        homes[0], picks, queries, fetch(0), per_grp, heads, jnp.stack(parts), jnp.stack(sizes)
    )[0]


def solution(mesh):
    in_specs = (
        P(("grp", "ctx"), None),
        P(("grp", "ctx"), None, None),
        P(("grp", "ctx"), None, None),
        P(("grp", "ctx"), None),
        P(),
    )
    out_specs = P(("grp", "ctx"), None)
    return jax.shard_map(
        on_device, mesh=mesh, in_specs=in_specs, out_specs=out_specs, check_vma=False
    )
```

```python
import functools
import math

import jax
import jax.numpy as jnp
from jax import lax
from jax.experimental import pallas as pl
from jax.experimental.pallas import tpu as pltpu
from jax.sharding import PartitionSpec as P


LANES = 128
LOG2E = math.log2(math.e)


def shifted(block, axis, distance):
    devices = range(lax.axis_size(axis))
    route = [((i - distance) % len(devices), i) for i in devices]
    return lax.ppermute(block, axis, route)


def plan_body(groups, ctx_count, cap, shift, place, lists, sends, places):
    group, here = place[0], place[1]
    rows = groups * ctx_count
    lane = lax.broadcasted_iota(jnp.int32, (rows, LANES), 1)
    earlier = (
        lax.broadcasted_iota(jnp.int32, (LANES, LANES), 0)
        < lax.broadcasted_iota(jnp.int32, (LANES, LANES), 1)
    ).astype(jnp.float32).astype(jnp.bfloat16)

    def rank_of(mask):
        ones = jnp.where(mask, 1.0, 0.0).astype(jnp.bfloat16)
        return jnp.dot(ones, earlier, preferred_element_type=jnp.float32).astype(jnp.int32)

    pages = lists[...]
    mine = (pages >> shift) == group * ctx_count + here
    rank = rank_of(mine)
    within = pages & ((1 << shift) - 1)
    found = jnp.full((rows, LANES), -1, jnp.int32)
    for k in range(cap):
        chosen = jnp.max(jnp.where(mine & (rank == k), within, -1), axis=1, keepdims=True)
        found = jnp.where(lane == k, chosen, found)
    sends[...] = found

    offset = lax.broadcasted_iota(jnp.int32, (ctx_count, LANES), 0)
    owner = here - offset
    owner = jnp.where(owner < 0, owner + ctx_count, owner)
    order = lax.broadcasted_iota(jnp.int32, (LANES, LANES), 0)
    for home in range(groups):
        listed = jnp.broadcast_to(lists[pl.ds(home * ctx_count + here, 1), :], (ctx_count, LANES))
        member = (listed >> shift) == group * ctx_count + owner
        slot = jnp.where(member, offset * cap + rank_of(member) + 1, 0)
        slot = jnp.broadcast_to(jnp.sum(slot, axis=0, keepdims=True) - 1, (LANES, LANES))
        inside = jnp.broadcast_to(slot[0:1] >= 0, (8, LANES))
        ordinal = (rank_of(inside) + 1).astype(jnp.float32).astype(jnp.bfloat16)
        onehot = jnp.where(slot == order, 1.0, 0.0).astype(jnp.bfloat16)
        position = lax.dot_general(
            ordinal, onehot, (((1,), (1,)), ((), ())), preferred_element_type=jnp.float32
        )
        places[home : home + 1, :] = position[0:1].astype(jnp.int32) - 1


def make_plan(place, lists, groups, ctx_count, cap, pages_here):
    rows = groups * ctx_count
    shift = pages_here.bit_length() - 1
    return pl.pallas_call(
        functools.partial(plan_body, groups, ctx_count, cap, shift),
        out_shape=(
            jax.ShapeDtypeStruct((rows, LANES), jnp.int32),
            jax.ShapeDtypeStruct((groups, LANES), jnp.int32),
        ),
        in_specs=[
            pl.BlockSpec(memory_space=pltpu.SMEM),
            pl.BlockSpec(memory_space=pltpu.VMEM),
        ],
        name="plan",
    )(place, lists)


def collect_body(ctx_count, cap, home, sends, keys, values, *rest):
    outs, sem = rest[:-1], rest[-1]
    here = home[1]

    def each(k, act):
        row = home[0] * ctx_count + lax.rem(here + k, ctx_count)

        def step(j, carry):
            page = sends[row, j]

            @pl.when(page >= 0)
            def _():
                act(pltpu.make_async_copy(keys.at[page], outs[k - 1].at[j, 0], sem))
                act(pltpu.make_async_copy(values.at[page], outs[k - 1].at[j, 1], sem))

            return carry

        lax.fori_loop(0, cap, step, 0)

    for k in range(1, ctx_count):
        each(k, lambda copy: copy.start())
    for k in range(1, ctx_count):
        each(k, lambda copy: copy.wait())


def collect(home, sends, keys, values, ctx_count, cap):
    _, block, hd = keys.shape
    peers = ctx_count - 1
    return pl.pallas_call(
        functools.partial(collect_body, ctx_count, cap),
        out_shape=(jax.ShapeDtypeStruct((cap, 2, block, hd), keys.dtype),) * peers,
        grid_spec=pltpu.PrefetchScalarGridSpec(
            num_scalar_prefetch=2,
            grid=(),
            in_specs=[pl.BlockSpec(memory_space=pl.ANY)] * 2,
            out_specs=(pl.BlockSpec(memory_space=pltpu.VMEM),) * peers,
            scratch_shapes=[pltpu.SemaphoreType.DMA(())],
        ),
        name="collect",
    )(home, sends, keys, values)


def attend_body(per_grp, heads, others, ctx_count, cap, home, places, sends, q, keys, values, *rest):
    arrived, rest = rest[: ctx_count - 1], rest[ctx_count - 1 :]
    if others:
        parts, sizes, out, kbuf, vbuf, sem = rest
    else:
        out, size_out, kbuf, vbuf, sem = rest
    tile = pl.program_id(0)
    block = q.shape[0]
    hd = q.shape[1] // heads
    span_keys = per_grp * block

    @pl.when(tile == 0)
    def _():
        own_row = home[0] * ctx_count + home[1]

        def load(k, j):
            position = places[home[0], k * cap + j]

            @pl.when(position >= 0)
            def _():
                which = position // per_grp
                span = pl.ds(pl.multiple_of(position * block, block), block)
                if k == 0:
                    page = sends[own_row, j]
                    key, value = keys.at[page], values.at[page]
                else:
                    key, value = arrived[k - 1].at[j, 0], arrived[k - 1].at[j, 1]
                pltpu.make_async_copy(key, kbuf.at[span], sem.at[which]).start()
                pltpu.make_async_copy(value, vbuf.at[span, pl.ds(0, hd)], sem.at[which]).start()

        for k in range(ctx_count):
            lax.fori_loop(0, cap, lambda j, carry, k=k: (load(k, j), carry)[1], 0)
        vbuf[:, hd:] = jnp.ones((vbuf.shape[0], hd), vbuf.dtype)

    here = pl.ds(pl.multiple_of(tile * span_keys, block), span_keys)
    for _ in range(per_grp):
        pltpu.make_async_copy(keys.at[0], kbuf.at[pl.ds(0, block)], sem.at[tile]).wait()
        pltpu.make_async_copy(values.at[0], vbuf.at[pl.ds(0, block), pl.ds(0, hd)], sem.at[tile]).wait()

    factor = hd ** (-0.5) * LOG2E
    diagonal = lax.broadcasted_iota(jnp.int32, (block, block), 0) == lax.broadcasted_iota(
        jnp.int32, (block, block), 1
    )
    pair = 2
    if others:
        size_rows = [sizes[g] for g in range(others)]
        size_cols = [jnp.transpose(rows) for rows in size_rows]
    for first in range(0, heads, pair):
        rows = jnp.concatenate([q[:, (first + i) * hd : (first + i + 1) * hd] for i in range(pair)], axis=0)
        scores = lax.dot_general(
            rows, kbuf[here, :], (((1,), (1,)), ((), ())), preferred_element_type=jnp.float32
        )
        top = jnp.max(scores, axis=1, keepdims=True)
        weights = jnp.exp2((scores - top) * factor).astype(jnp.bfloat16)
        summed = jnp.dot(weights, vbuf[here, :], preferred_element_type=jnp.float32)
        for i in range(pair):
            span = slice(i * block, (i + 1) * block)
            col = slice((first + i) * hd, (first + i + 1) * hd)
            total = summed[span, hd:]
            mine = summed[span, :hd] / total
            size = top[span] * factor + jnp.log2(total)
            if others:
                theirs = [
                    jnp.broadcast_to(size_cols[g][:, first + i : first + i + 1], (block, hd))
                    for g in range(others)
                ]
                peak = size
                for one in theirs:
                    peak = jnp.maximum(peak, one)
                share = jnp.exp2(size - peak)
                whole = share
                merged = mine * share
                for g in range(others):
                    share = jnp.exp2(theirs[g] - peak)
                    whole = whole + share
                    merged = merged + parts[g, :, col].astype(jnp.float32) * share
                out[:, col] = (merged / whole).astype(out.dtype)
            else:
                out[:, col] = mine.astype(out.dtype)
                size_out[0, first + i : first + i + 1, :] = jnp.sum(
                    jnp.where(diagonal, size, 0.0), axis=0, keepdims=True
                )


def attend(home, places, sends, q, keys, values, arrived, per_grp, cap, heads, parts=None, sizes=None):
    tokens, width = q.shape
    block, hd = keys.shape[1:]
    tiles = tokens // block
    ctx_count = len(arrived) + 1
    others = 0 if parts is None else parts.shape[0]
    q_spec = pl.BlockSpec((block, width), lambda t, *_: (t, 0))
    size_shape = (heads, block)
    in_specs = [q_spec] + [pl.BlockSpec(memory_space=pl.ANY)] * (ctx_count + 1)
    operands = [q, keys, values, *arrived]
    out_shape = [jax.ShapeDtypeStruct((tokens, width), q.dtype)]
    out_specs = [q_spec]
    if others:
        in_specs += [
            pl.BlockSpec((others, block, width), lambda t, *_: (0, t, 0)),
            pl.BlockSpec((others, None) + size_shape, lambda t, *_: (0, t, 0, 0)),
        ]
        operands += [parts, sizes]
    else:
        out_shape.append(jax.ShapeDtypeStruct((tiles,) + size_shape, jnp.float32))
        out_specs.append(pl.BlockSpec((1,) + size_shape, lambda t, *_: (t, 0, 0)))
    return pl.pallas_call(
        functools.partial(attend_body, per_grp, heads, others, ctx_count, cap),
        out_shape=tuple(out_shape),
        grid_spec=pltpu.PrefetchScalarGridSpec(
            num_scalar_prefetch=3,
            grid=(tiles,),
            in_specs=in_specs,
            out_specs=tuple(out_specs),
            scratch_shapes=[
                pltpu.VMEM((tiles * per_grp * block, hd), q.dtype),
                pltpu.VMEM((tiles * per_grp * block, 2 * hd), q.dtype),
                pltpu.SemaphoreType.DMA((tiles,)),
            ],
        ),
        compiler_params=pltpu.CompilerParams(vmem_limit_bytes=48 * 1024 * 1024),
        name="attend_last" if others else "attend",
    )(home, places, sends, *operands)


def on_device(queries, keys_cache, values_cache, block_list, page_table):
    groups = lax.axis_size("grp")
    ctx_count = lax.axis_size("ctx")
    tile_count, listed = block_list.shape
    pages_here, _, hd = keys_cache.shape
    heads = queries.shape[1] // hd
    per_grp = listed // groups
    cap = max(3, (2 * tile_count * per_grp + ctx_count - 1) // ctx_count)
    group_here = lax.axis_index("grp")
    ctx_here = lax.axis_index("ctx")
    place = jnp.stack([group_here, ctx_here]).astype(jnp.int32)

    page_ids = page_table[block_list].reshape(1, tile_count * listed)
    page_ids = jnp.pad(page_ids, ((0, 0), (0, LANES - tile_count * listed)), constant_values=-1)
    everywhere = jnp.broadcast_to(page_ids, (groups * ctx_count, LANES))
    lists = lax.all_to_all(everywhere, ("grp", "ctx"), split_axis=0, concat_axis=0, tiled=True)
    sends, places = make_plan(place, lists, groups, ctx_count, cap, pages_here)

    shifts = visit_order(groups)
    homes = [jnp.stack([(group_here - s) % groups, ctx_here]).astype(jnp.int32) for s in shifts]
    visiting = []
    for s in shifts[:-1]:
        visiting.append(shifted(queries, "grp", s))
    visiting.append(queries)

    parts, sizes = [], []
    for r, s in enumerate(shifts):
        gathered = collect(homes[r], sends, keys_cache, values_cache, ctx_count, cap)
        arrived = []
        for k in range(1, ctx_count):
            arrived.append(shifted(gathered[k - 1], "ctx", k))
        local = (homes[r], places, sends, visiting[r], keys_cache, values_cache, arrived)
        if s:
            part, size = attend(*local, per_grp, cap, heads)
            parts.append(shifted(part, "grp", -s))
            sizes.append(shifted(size, "grp", -s))
    return attend(*local, per_grp, cap, heads, jnp.stack(parts), jnp.stack(sizes))[0]


def visit_order(groups):
    middle = groups // 2
    return [middle] + [s for s in range(1, groups) if s != middle] + [0]


def solution(mesh):
    in_specs = (
        P(("grp", "ctx"), None),
        P(("grp", "ctx"), None, None),
        P(("grp", "ctx"), None, None),
        P(("grp", "ctx"), None),
        P(),
    )
    out_specs = P(("grp", "ctx"), None)

    return jax.shard_map(on_device, mesh=mesh, in_specs=in_specs, out_specs=out_specs, check_vma=False)
```

```python
import functools
import math

import jax
import jax.numpy as jnp
from jax import lax
from jax.experimental import pallas as pl
from jax.experimental.pallas import tpu as pltpu
from jax.sharding import PartitionSpec as P


LANES = 128
LOG2E = math.log2(math.e)


def shifted(block, axis, distance):
    devices = range(lax.axis_size(axis))
    route = [((i - distance) % len(devices), i) for i in devices]
    return lax.ppermute(block, axis, route)


def plan_body(groups, ctx_count, cap, shift, place, lists, sends, places):
    group, here = place[0], place[1]
    rows = groups * ctx_count
    lane = lax.broadcasted_iota(jnp.int32, (rows, LANES), 1)
    earlier = (
        lax.broadcasted_iota(jnp.int32, (LANES, LANES), 0)
        < lax.broadcasted_iota(jnp.int32, (LANES, LANES), 1)
    ).astype(jnp.float32).astype(jnp.bfloat16)

    def rank_of(mask):
        ones = jnp.where(mask, 1.0, 0.0).astype(jnp.bfloat16)
        return jnp.dot(ones, earlier, preferred_element_type=jnp.float32).astype(jnp.int32)

    pages = lists[...]
    mine = (pages >> shift) == group * ctx_count + here
    rank = rank_of(mine)
    within = pages & ((1 << shift) - 1)
    found = jnp.full((rows, LANES), -1, jnp.int32)
    for k in range(cap):
        chosen = jnp.max(jnp.where(mine & (rank == k), within, -1), axis=1, keepdims=True)
        found = jnp.where(lane == k, chosen, found)
    sends[...] = found

    offset = lax.broadcasted_iota(jnp.int32, (ctx_count, LANES), 0)
    owner = here - offset
    owner = jnp.where(owner < 0, owner + ctx_count, owner)
    order = lax.broadcasted_iota(jnp.int32, (LANES, LANES), 0)
    for home in range(groups):
        listed = jnp.broadcast_to(lists[pl.ds(home * ctx_count + here, 1), :], (ctx_count, LANES))
        member = (listed >> shift) == group * ctx_count + owner
        slot = jnp.where(member, offset * cap + rank_of(member) + 1, 0)
        slot = jnp.broadcast_to(jnp.sum(slot, axis=0, keepdims=True) - 1, (LANES, LANES))
        inside = jnp.broadcast_to(slot[0:1] >= 0, (8, LANES))
        ordinal = (rank_of(inside) + 1).astype(jnp.float32).astype(jnp.bfloat16)
        onehot = jnp.where(slot == order, 1.0, 0.0).astype(jnp.bfloat16)
        position = lax.dot_general(
            ordinal, onehot, (((1,), (1,)), ((), ())), preferred_element_type=jnp.float32
        )
        places[home : home + 1, :] = position[0:1].astype(jnp.int32) - 1


def make_plan(place, lists, groups, ctx_count, cap, pages_here):
    rows = groups * ctx_count
    shift = pages_here.bit_length() - 1
    return pl.pallas_call(
        functools.partial(plan_body, groups, ctx_count, cap, shift),
        out_shape=(
            jax.ShapeDtypeStruct((rows, LANES), jnp.int32),
            jax.ShapeDtypeStruct((groups, LANES), jnp.int32),
        ),
        in_specs=[
            pl.BlockSpec(memory_space=pltpu.SMEM),
            pl.BlockSpec(memory_space=pltpu.VMEM),
        ],
        name="plan",
    )(place, lists)


def collect_body(ctx_count, cap, home, sends, keys, values, *rest):
    outs, sem = rest[:-1], rest[-1]
    here = home[1]

    def each(k, act):
        row = home[0] * ctx_count + lax.rem(here + k, ctx_count)

        def step(j, carry):
            page = sends[row, j]

            @pl.when(page >= 0)
            def _():
                act(pltpu.make_async_copy(keys.at[page], outs[k - 1].at[j, 0], sem))
                act(pltpu.make_async_copy(values.at[page], outs[k - 1].at[j, 1], sem))

            return carry

        lax.fori_loop(0, cap, step, 0)

    for k in range(1, ctx_count):
        each(k, lambda copy: copy.start())
    for k in range(1, ctx_count):
        each(k, lambda copy: copy.wait())


def collect(home, sends, keys, values, ctx_count, cap):
    _, block, hd = keys.shape
    peers = ctx_count - 1
    return pl.pallas_call(
        functools.partial(collect_body, ctx_count, cap),
        out_shape=(jax.ShapeDtypeStruct((cap, 2, block, hd), keys.dtype),) * peers,
        grid_spec=pltpu.PrefetchScalarGridSpec(
            num_scalar_prefetch=2,
            grid=(),
            in_specs=[pl.BlockSpec(memory_space=pl.ANY)] * 2,
            out_specs=(pl.BlockSpec(memory_space=pltpu.VMEM),) * peers,
            scratch_shapes=[pltpu.SemaphoreType.DMA(())],
        ),
        name="collect",
    )(home, sends, keys, values)


def attend_body(per_grp, heads, others, ctx_count, cap, home, places, sends, q, keys, values, *rest):
    arrived, rest = rest[: ctx_count - 1], rest[ctx_count - 1 :]
    parts, sizes = rest[:others], rest[others : 2 * others]
    rest = rest[2 * others :]
    if others:
        out, kbuf, vbuf, sem = rest
    else:
        out, size_out, kbuf, vbuf, sem = rest
    tile = pl.program_id(0)
    block = q.shape[0]
    hd = q.shape[1] // heads
    span_keys = per_grp * block

    @pl.when(tile == 0)
    def _():
        own_row = home[0] * ctx_count + home[1]

        def load(k, j):
            position = places[home[0], k * cap + j]

            @pl.when(position >= 0)
            def _():
                which = position // per_grp
                span = pl.ds(pl.multiple_of(position * block, block), block)
                if k == 0:
                    page = sends[own_row, j]
                    key, value = keys.at[page], values.at[page]
                else:
                    key, value = arrived[k - 1].at[j, 0], arrived[k - 1].at[j, 1]
                pltpu.make_async_copy(key, kbuf.at[span], sem.at[which]).start()
                pltpu.make_async_copy(value, vbuf.at[span, pl.ds(0, hd)], sem.at[which]).start()

        for k in range(ctx_count):
            lax.fori_loop(0, cap, lambda j, carry, k=k: (load(k, j), carry)[1], 0)
        vbuf[:, hd:] = jnp.ones((vbuf.shape[0], hd), vbuf.dtype)

    here = pl.ds(pl.multiple_of(tile * span_keys, block), span_keys)
    for _ in range(per_grp):
        pltpu.make_async_copy(keys.at[0], kbuf.at[pl.ds(0, block)], sem.at[tile]).wait()
        pltpu.make_async_copy(values.at[0], vbuf.at[pl.ds(0, block), pl.ds(0, hd)], sem.at[tile]).wait()

    factor = hd ** (-0.5) * LOG2E
    diagonal = lax.broadcasted_iota(jnp.int32, (block, block), 0) == lax.broadcasted_iota(
        jnp.int32, (block, block), 1
    )
    pair = 2
    if others:
        size_cols = [jnp.transpose(sizes[g][...]) for g in range(others)]
    for first in range(0, heads, pair):
        rows = jnp.concatenate([q[:, (first + i) * hd : (first + i + 1) * hd] for i in range(pair)], axis=0)
        scores = lax.dot_general(
            rows, kbuf[here, :], (((1,), (1,)), ((), ())), preferred_element_type=jnp.float32
        )
        top = jnp.max(scores, axis=1, keepdims=True)
        weights = jnp.exp2((scores - top) * factor).astype(jnp.bfloat16)
        summed = jnp.dot(weights, vbuf[here, :], preferred_element_type=jnp.float32)
        for i in range(pair):
            span = slice(i * block, (i + 1) * block)
            col = slice((first + i) * hd, (first + i + 1) * hd)
            total = summed[span, hd:]
            mine = summed[span, :hd] / total
            size = top[span] * factor + jnp.log2(total)
            if others:
                theirs = [
                    jnp.broadcast_to(size_cols[g][:, first + i : first + i + 1], (block, hd))
                    for g in range(others)
                ]
                peak = size
                for one in theirs:
                    peak = jnp.maximum(peak, one)
                share = jnp.exp2(size - peak)
                whole = share
                merged = mine * share
                for g in range(others):
                    share = jnp.exp2(theirs[g] - peak)
                    whole = whole + share
                    merged = merged + parts[g][:, col].astype(jnp.float32) * share
                out[:, col] = (merged / whole).astype(out.dtype)
            else:
                out[:, col] = mine.astype(out.dtype)
                size_out[0, first + i : first + i + 1, :] = jnp.sum(
                    jnp.where(diagonal, size, 0.0), axis=0, keepdims=True
                )


def attend(home, places, sends, q, keys, values, arrived, per_grp, cap, heads, parts=(), sizes=()):
    tokens, width = q.shape
    block, hd = keys.shape[1:]
    tiles = tokens // block
    ctx_count = len(arrived) + 1
    others = len(parts)
    q_spec = pl.BlockSpec((block, width), lambda t, *_: (t, 0))
    size_shape = (heads, block)
    in_specs = [q_spec] + [pl.BlockSpec(memory_space=pl.ANY)] * (ctx_count + 1)
    operands = [q, keys, values, *arrived]
    out_shape = [jax.ShapeDtypeStruct((tokens, width), q.dtype)]
    out_specs = [q_spec]
    if others:
        in_specs += [q_spec] * others
        in_specs += [pl.BlockSpec((None,) + size_shape, lambda t, *_: (t, 0, 0))] * others
        operands += [*parts, *sizes]
    else:
        out_shape.append(jax.ShapeDtypeStruct((tiles,) + size_shape, jnp.float32))
        out_specs.append(pl.BlockSpec((1,) + size_shape, lambda t, *_: (t, 0, 0)))
    return pl.pallas_call(
        functools.partial(attend_body, per_grp, heads, others, ctx_count, cap),
        out_shape=tuple(out_shape),
        grid_spec=pltpu.PrefetchScalarGridSpec(
            num_scalar_prefetch=3,
            grid=(tiles,),
            in_specs=in_specs,
            out_specs=tuple(out_specs),
            scratch_shapes=[
                pltpu.VMEM((tiles * per_grp * block, hd), q.dtype),
                pltpu.VMEM((tiles * per_grp * block, 2 * hd), q.dtype),
                pltpu.SemaphoreType.DMA((tiles,)),
            ],
        ),
        compiler_params=pltpu.CompilerParams(vmem_limit_bytes=48 * 1024 * 1024),
        name="attend_last" if others else "attend",
    )(home, places, sends, *operands)


def on_device(queries, keys_cache, values_cache, block_list, page_table):
    groups = lax.axis_size("grp")
    ctx_count = lax.axis_size("ctx")
    tile_count, listed = block_list.shape
    pages_here, _, hd = keys_cache.shape
    heads = queries.shape[1] // hd
    per_grp = listed // groups
    cap = max(3, (2 * tile_count * per_grp + ctx_count - 1) // ctx_count)
    group_here = lax.axis_index("grp")
    ctx_here = lax.axis_index("ctx")
    place = jnp.stack([group_here, ctx_here]).astype(jnp.int32)

    page_ids = page_table[block_list].reshape(1, tile_count * listed)
    page_ids = jnp.pad(page_ids, ((0, 0), (0, LANES - tile_count * listed)), constant_values=-1)
    everywhere = jnp.broadcast_to(page_ids, (groups * ctx_count, LANES))
    lists = lax.all_to_all(everywhere, ("grp", "ctx"), split_axis=0, concat_axis=0, tiled=True)
    sends, places = make_plan(place, lists, groups, ctx_count, cap, pages_here)

    shifts = visit_order(groups)
    homes = [jnp.stack([(group_here - s) % groups, ctx_here]).astype(jnp.int32) for s in shifts]
    visiting = []
    for s in shifts[:-1]:
        visiting.append(shifted(queries, "grp", s))
    visiting.append(queries)

    parts, sizes = [], []
    for r, s in enumerate(shifts):
        gathered = collect(homes[r], sends, keys_cache, values_cache, ctx_count, cap)
        arrived = []
        for k in range(1, ctx_count):
            arrived.append(shifted(gathered[k - 1], "ctx", k))
        local = (homes[r], places, sends, visiting[r], keys_cache, values_cache, arrived)
        if s:
            part, size = attend(*local, per_grp, cap, heads)
            parts.append(shifted(part, "grp", -s))
            sizes.append(shifted(size, "grp", -s))
    return attend(*local, per_grp, cap, heads, parts, sizes)[0]


def visit_order(groups):
    middle = groups // 2
    return [middle] + [s for s in range(1, groups) if s != middle] + [0]


def solution(mesh):
    in_specs = (
        P(("grp", "ctx"), None),
        P(("grp", "ctx"), None, None),
        P(("grp", "ctx"), None, None),
        P(("grp", "ctx"), None),
        P(),
    )
    out_specs = P(("grp", "ctx"), None)

    return jax.shard_map(on_device, mesh=mesh, in_specs=in_specs, out_specs=out_specs, check_vma=False)
```

```python
import functools
import math

import jax
import jax.numpy as jnp
from jax import lax
from jax.experimental import pallas as pl
from jax.experimental.pallas import tpu as pltpu
from jax.sharding import PartitionSpec as P


LANES = 128
LOG2E = math.log2(math.e)


def shifted(block, axis, distance):
    devices = range(lax.axis_size(axis))
    route = [((i - distance) % len(devices), i) for i in devices]
    return lax.ppermute(block, axis, route)


def plan_body(groups, ctx_count, cap, shift, place, lists, sends, places):
    group, here = place[0], place[1]
    rows = groups * ctx_count
    lane = lax.broadcasted_iota(jnp.int32, (rows, LANES), 1)
    earlier = (
        lax.broadcasted_iota(jnp.int32, (LANES, LANES), 0)
        < lax.broadcasted_iota(jnp.int32, (LANES, LANES), 1)
    ).astype(jnp.float32).astype(jnp.bfloat16)

    def rank_of(mask):
        ones = jnp.where(mask, 1.0, 0.0).astype(jnp.bfloat16)
        return jnp.dot(ones, earlier, preferred_element_type=jnp.float32).astype(jnp.int32)

    pages = lists[...]
    mine = (pages >> shift) == group * ctx_count + here
    rank = rank_of(mine)
    within = pages & ((1 << shift) - 1)
    found = jnp.full((rows, LANES), -1, jnp.int32)
    for k in range(cap):
        chosen = jnp.max(jnp.where(mine & (rank == k), within, -1), axis=1, keepdims=True)
        found = jnp.where(lane == k, chosen, found)
    sends[...] = found

    offset = lax.broadcasted_iota(jnp.int32, (ctx_count, LANES), 0)
    owner = here - offset
    owner = jnp.where(owner < 0, owner + ctx_count, owner)
    order = lax.broadcasted_iota(jnp.int32, (LANES, LANES), 0)
    for home in range(groups):
        listed = jnp.broadcast_to(lists[pl.ds(home * ctx_count + here, 1), :], (ctx_count, LANES))
        member = (listed >> shift) == group * ctx_count + owner
        slot = jnp.where(member, offset * cap + rank_of(member) + 1, 0)
        slot = jnp.broadcast_to(jnp.sum(slot, axis=0, keepdims=True) - 1, (LANES, LANES))
        inside = jnp.broadcast_to(slot[0:1] >= 0, (8, LANES))
        ordinal = (rank_of(inside) + 1).astype(jnp.float32).astype(jnp.bfloat16)
        onehot = jnp.where(slot == order, 1.0, 0.0).astype(jnp.bfloat16)
        position = lax.dot_general(
            ordinal, onehot, (((1,), (1,)), ((), ())), preferred_element_type=jnp.float32
        )
        places[home : home + 1, :] = position[0:1].astype(jnp.int32) - 1


def make_plan(place, lists, groups, ctx_count, cap, pages_here):
    rows = groups * ctx_count
    shift = pages_here.bit_length() - 1
    return pl.pallas_call(
        functools.partial(plan_body, groups, ctx_count, cap, shift),
        out_shape=(
            jax.ShapeDtypeStruct((rows, LANES), jnp.int32),
            jax.ShapeDtypeStruct((groups, LANES), jnp.int32),
        ),
        in_specs=[
            pl.BlockSpec(memory_space=pltpu.SMEM),
            pl.BlockSpec(memory_space=pltpu.VMEM),
        ],
        name="plan",
    )(place, lists)


def collect_body(ctx_count, cap, split, home, sends, keys, values, *rest):
    outs, (stage, sem_in, sem_out) = rest[:-3], rest[-3:]
    here = home[1]
    peers = ctx_count - 1

    def each(k, act):
        row = home[0] * ctx_count + lax.rem(here + k, ctx_count)

        def step(j, carry):
            page = sends[row, j]

            @pl.when(page >= 0)
            def _():
                act(page, j, (k - 1) * cap + j)

            return carry

        lax.fori_loop(0, cap, step, 0)

    def incoming(page, place):
        return (
            pltpu.make_async_copy(keys.at[page], stage.at[place, 0], sem_in.at[place]),
            pltpu.make_async_copy(values.at[page], stage.at[place, 1], sem_in.at[place]),
        )

    def outgoing(k, j, place):
        if split:
            return (
                pltpu.make_async_copy(stage.at[place, 0], outs[k - 1].at[j], sem_out),
                pltpu.make_async_copy(stage.at[place, 1], outs[peers + k - 1].at[j], sem_out),
            )
        return (pltpu.make_async_copy(stage.at[place], outs[k - 1].at[j], sem_out),)

    def fetch(page, j, place):
        for copy in incoming(page, place):
            copy.start()

    for k in range(1, ctx_count):
        each(k, fetch)
    for k in range(1, ctx_count):

        def forward(page, j, place, k=k):
            for copy in incoming(page, place):
                copy.wait()
            for copy in outgoing(k, j, place):
                copy.start()

        each(k, forward)
    for k in range(1, ctx_count):

        def finish(page, j, place, k=k):
            for copy in outgoing(k, j, place):
                copy.wait()

        each(k, finish)


def collect(home, sends, keys, values, ctx_count, cap, split):
    _, block, hd = keys.shape
    peers = ctx_count - 1
    if split:
        shapes = (jax.ShapeDtypeStruct((cap, block, hd), keys.dtype),) * (2 * peers)
    else:
        shapes = (jax.ShapeDtypeStruct((cap, 2, block, hd), keys.dtype),) * peers
    return pl.pallas_call(
        functools.partial(collect_body, ctx_count, cap, split),
        out_shape=shapes,
        grid_spec=pltpu.PrefetchScalarGridSpec(
            num_scalar_prefetch=2,
            grid=(),
            in_specs=[pl.BlockSpec(memory_space=pl.ANY)] * 2,
            out_specs=(pl.BlockSpec(memory_space=pl.ANY),) * len(shapes),
            scratch_shapes=[
                pltpu.VMEM((peers * cap, 2, block, hd), keys.dtype),
                pltpu.SemaphoreType.DMA((peers * cap,)),
                pltpu.SemaphoreType.DMA(()),
            ],
        ),
        name="collect",
    )(home, sends, keys, values)


def load_pages(per_grp, ctx_count, cap, home, places, sends, sources, buffers, sem):
    block, hd = sources[0][0].shape[1:]
    own_row = home[0] * ctx_count + home[1]

    def load(k, j):
        position = places[home[0], k * cap + j]

        @pl.when(position >= 0)
        def _():
            which = position // per_grp
            span = pl.ds(pl.multiple_of(position * block, block), block)
            for source, buffer in zip(sources, buffers):
                origin = source[0].at[sends[own_row, j]] if k == 0 else source[k](j)
                pltpu.make_async_copy(origin, buffer.at[span, pl.ds(0, hd)], sem.at[which]).start()

    for k in range(ctx_count):
        lax.fori_loop(0, cap, lambda j, carry, k=k: (load(k, j), carry)[1], 0)


def wait_pages(per_grp, sources, buffers, tile, sem):
    block, hd = sources[0][0].shape[1:]
    for _ in range(per_grp):
        for source, buffer in zip(sources, buffers):
            pltpu.make_async_copy(
                source[0].at[0], buffer.at[pl.ds(0, block), pl.ds(0, hd)], sem.at[tile]
            ).wait()


def head_rows(q, first, pair, hd):
    return jnp.concatenate([q[:, (first + i) * hd : (first + i + 1) * hd] for i in range(pair)], axis=0)


def weigh(rows, keys_now, factor):
    scores = lax.dot_general(
        rows, keys_now, (((1,), (1,)), ((), ())), preferred_element_type=jnp.float32
    )
    top = jnp.max(scores, axis=1, keepdims=True)
    return jnp.exp2((scores - top) * factor).astype(jnp.bfloat16), top * factor


def as_row(column, diagonal):
    return jnp.sum(jnp.where(diagonal, column, 0.0), axis=0, keepdims=True)


def diagonal_of(block):
    rows = lax.broadcasted_iota(jnp.int32, (block, block), 0)
    return rows == lax.broadcasted_iota(jnp.int32, (block, block), 1)


PAIR = 2


def attend_body(per_grp, heads, ctx_count, cap, home, places, sends, q, keys, values, *rest):
    arrived, (out, size_out, kbuf, vbuf, sem) = rest[: ctx_count - 1], rest[ctx_count - 1 :]
    tile = pl.program_id(0)
    block = q.shape[0]
    hd = q.shape[1] // heads
    sources = [
        [cache] + [lambda j, one=one, part=part: one.at[j, part] for one in arrived]
        for part, cache in enumerate((keys, values))
    ]
    buffers = (kbuf, vbuf)

    @pl.when(tile == 0)
    def _():
        load_pages(per_grp, ctx_count, cap, home, places, sends, sources, buffers, sem)
        vbuf[:, hd:] = jnp.ones((vbuf.shape[0], hd), vbuf.dtype)

    here = pl.ds(pl.multiple_of(tile * per_grp * block, block), per_grp * block)
    wait_pages(per_grp, sources, buffers, tile, sem)
    factor = hd ** (-0.5) * LOG2E
    diagonal = diagonal_of(block)
    for first in range(0, heads, PAIR):
        weights, top = weigh(head_rows(q, first, PAIR, hd), kbuf[here, :], factor)
        summed = jnp.dot(weights, vbuf[here, :], preferred_element_type=jnp.float32)
        for i in range(PAIR):
            span = slice(i * block, (i + 1) * block)
            total = summed[span, hd:]
            out[:, (first + i) * hd : (first + i + 1) * hd] = (summed[span, :hd] / total).astype(out.dtype)
            size_out[0, first + i : first + i + 1, :] = as_row(top[span] + jnp.log2(total), diagonal)


def score_body(per_grp, heads, ctx_count, cap, home, places, sends, q, keys, *rest):
    arrived, (out, top_out, kbuf, sem) = rest[: ctx_count - 1], rest[ctx_count - 1 :]
    tile = pl.program_id(0)
    block = q.shape[0]
    hd = q.shape[1] // heads
    sources = [[keys] + [lambda j, one=one: one.at[j] for one in arrived]]

    @pl.when(tile == 0)
    def _():
        load_pages(per_grp, ctx_count, cap, home, places, sends, sources, (kbuf,), sem)

    here = pl.ds(pl.multiple_of(tile * per_grp * block, block), per_grp * block)
    wait_pages(per_grp, sources, (kbuf,), tile, sem)
    diagonal = diagonal_of(block)
    for first in range(0, heads, PAIR):
        rows = head_rows(q, first, PAIR, hd)
        weights, top = weigh(rows, kbuf[here, :], hd ** (-0.5) * LOG2E)
        out[0, first * block : (first + PAIR) * block, :] = weights
        for i in range(PAIR):
            top_out[0, first + i : first + i + 1, :] = as_row(top[i * block : (i + 1) * block], diagonal)


def finish_body(per_grp, heads, ctx_count, cap, others, home, places, sends, weights, top, values, *rest):
    arrived, rest = rest[: ctx_count - 1], rest[ctx_count - 1 :]
    parts, sizes, (out, vbuf, sem) = rest[:others], rest[others : 2 * others], rest[2 * others :]
    tile = pl.program_id(0)
    block = out.shape[0]
    hd = out.shape[1] // heads
    sources = [[values] + [lambda j, one=one: one.at[j] for one in arrived]]

    @pl.when(tile == 0)
    def _():
        load_pages(per_grp, ctx_count, cap, home, places, sends, sources, (vbuf,), sem)
        vbuf[:, hd:] = jnp.ones((vbuf.shape[0], hd), vbuf.dtype)

    here = pl.ds(pl.multiple_of(tile * per_grp * block, block), per_grp * block)
    wait_pages(per_grp, sources, (vbuf,), tile, sem)
    columns = [jnp.transpose(one[...]) for one in (top,) + tuple(sizes)]
    for first in range(0, heads, PAIR):
        summed = jnp.dot(
            weights[first * block : (first + PAIR) * block, :],
            vbuf[here, :],
            preferred_element_type=jnp.float32,
        )
        for i in range(PAIR):
            span = slice(i * block, (i + 1) * block)
            col = slice((first + i) * hd, (first + i + 1) * hd)
            spread = [jnp.broadcast_to(one[:, first + i : first + i + 1], (block, hd)) for one in columns]
            peak = spread[0]
            for one in spread[1:]:
                peak = jnp.maximum(peak, one)
            share = jnp.exp2(spread[0] - peak)
            whole = summed[span, hd:] * share
            merged = summed[span, :hd] * share
            for part, one in zip(parts, spread[1:]):
                share = jnp.exp2(one - peak)
                whole = whole + share
                merged = merged + part[:, col].astype(jnp.float32) * share
            out[:, col] = (merged / whole).astype(out.dtype)


class Sizes:
    def __init__(self, tokens, block, hd, heads, per_grp, ctx_count, cap, dtype):
        self.block, self.hd, self.heads = block, hd, heads
        self.per_grp, self.ctx_count, self.cap = per_grp, ctx_count, cap
        self.tiles, self.dtype = tokens // block, dtype
        self.keys = per_grp * block
        self.row_spec = pl.BlockSpec((block, heads * hd), lambda t, *_: (t, 0))
        self.rows = jax.ShapeDtypeStruct((tokens, heads * hd), dtype)
        self.stat_spec = pl.BlockSpec((1, heads, block), lambda t, *_: (t, 0, 0))
        self.stat_in = pl.BlockSpec((None, heads, block), lambda t, *_: (t, 0, 0))
        self.stat = jax.ShapeDtypeStruct((self.tiles, heads, block), jnp.float32)

    def call(self, body, in_specs, out_shape, out_specs, buffers, operands, *extra):
        lead = (self.per_grp, self.heads, self.ctx_count, self.cap) + extra
        return pl.pallas_call(
            functools.partial(body, *lead),
            out_shape=out_shape,
            grid_spec=pltpu.PrefetchScalarGridSpec(
                num_scalar_prefetch=3,
                grid=(self.tiles,),
                in_specs=in_specs,
                out_specs=out_specs,
                scratch_shapes=[
                    pltpu.VMEM((self.tiles * self.keys, width), self.dtype) for width in buffers
                ]
                + [pltpu.SemaphoreType.DMA((self.tiles,))],
            ),
            compiler_params=pltpu.CompilerParams(vmem_limit_bytes=48 * 1024 * 1024),
        )(*operands)

    def attend(self, home, places, sends, q, keys, values, arrived):
        return self.call(
            attend_body,
            [self.row_spec] + [pl.BlockSpec(memory_space=pl.ANY)] * (self.ctx_count + 1),
            (self.rows, self.stat),
            (self.row_spec, self.stat_spec),
            (self.hd, 2 * self.hd),
            (home, places, sends, q, keys, values, *arrived),
        )

    def score(self, home, places, sends, q, keys, arrived):
        shape = (self.tiles, self.heads * self.block, self.keys)
        return self.call(
            score_body,
            [self.row_spec] + [pl.BlockSpec(memory_space=pl.ANY)] * self.ctx_count,
            (jax.ShapeDtypeStruct(shape, self.dtype), self.stat),
            (pl.BlockSpec((1,) + shape[1:], lambda t, *_: (t, 0, 0)), self.stat_spec),
            (self.hd,),
            (home, places, sends, q, keys, *arrived),
        )

    def finish(self, home, places, sends, weights, top, values, arrived, parts, sizes):
        return self.call(
            finish_body,
            [pl.BlockSpec((None,) + weights.shape[1:], lambda t, *_: (t, 0, 0)), self.stat_in]
            + [pl.BlockSpec(memory_space=pl.ANY)] * self.ctx_count
            + [self.row_spec] * len(parts)
            + [self.stat_in] * len(sizes),
            self.rows,
            self.row_spec,
            (2 * self.hd,),
            (home, places, sends, weights, top, values, *arrived, *parts, *sizes),
            len(parts),
        )


def on_device(queries, keys_cache, values_cache, block_list, page_table):
    groups = lax.axis_size("grp")
    ctx_count = lax.axis_size("ctx")
    tile_count, listed = block_list.shape
    pages_here, block, hd = keys_cache.shape
    heads = queries.shape[1] // hd
    per_grp = listed // groups
    cap = max(3, (2 * tile_count * per_grp + ctx_count - 1) // ctx_count)
    group_here = lax.axis_index("grp")
    ctx_here = lax.axis_index("ctx")
    place = jnp.stack([group_here, ctx_here]).astype(jnp.int32)
    kernels = Sizes(queries.shape[0], block, hd, heads, per_grp, ctx_count, cap, queries.dtype)

    page_ids = page_table[block_list].reshape(1, tile_count * listed)
    page_ids = jnp.pad(page_ids, ((0, 0), (0, LANES - tile_count * listed)), constant_values=-1)
    everywhere = jnp.broadcast_to(page_ids, (groups * ctx_count, LANES))
    lists = lax.all_to_all(everywhere, ("grp", "ctx"), split_axis=0, concat_axis=0, tiled=True)
    sends, places = make_plan(place, lists, groups, ctx_count, cap, pages_here)

    shifts = visit_order(groups)
    homes = [jnp.stack([(group_here - s) % groups, ctx_here]).astype(jnp.int32) for s in shifts]
    visiting = []
    for s in shifts[:-1]:
        visiting.append(shifted(queries, "grp", s))

    def gather(r, split):
        return collect(homes[r], sends, keys_cache, values_cache, ctx_count, cap, split)

    def swap(gathered):
        arrived = []
        for k in range(1, ctx_count):
            arrived.append(shifted(gathered[k - 1], "ctx", k))
        return arrived

    parts, sizes = [], []
    for r, s in enumerate(shifts[:-1]):
        arrived = swap(gather(r, False))
        part, size = kernels.attend(
            homes[r], places, sends, visiting[r], keys_cache, values_cache, arrived
        )
        parts.append(shifted(part, "grp", -s))
        sizes.append(shifted(size, "grp", -s))
    last = groups - 1
    gathered = gather(last, True)
    arrived_keys = swap(gathered[: ctx_count - 1])
    arrived_values = swap(gathered[ctx_count - 1 :])
    weights, top = kernels.score(homes[last], places, sends, queries, keys_cache, arrived_keys)
    return kernels.finish(
        homes[last], places, sends, weights, top, values_cache, arrived_values, parts, sizes
    )


def visit_order(groups):
    middle = groups // 2
    return [middle] + [s for s in range(1, groups) if s != middle] + [0]


def solution(mesh):
    in_specs = (
        P(("grp", "ctx"), None),
        P(("grp", "ctx"), None, None),
        P(("grp", "ctx"), None, None),
        P(("grp", "ctx"), None),
        P(),
    )
    out_specs = P(("grp", "ctx"), None)

    return jax.shard_map(on_device, mesh=mesh, in_specs=in_specs, out_specs=out_specs, check_vma=False)
```
